32 devices in a mesh: node: 32 (over z, y, x, core), rel: 1.
Axes of the slice: x: 2, y: 2, z: 4, core: 2. Of those that a mesh axis runs over, the one named last changes fastest.
Arguments:
- features: bfloat16 [1, 512, 768], P('rel', 'node'), may hold values from -6 to 6
- bases: bfloat16 [30, 768, 1024], P(None, 'node', 'rel'), may hold values from -0.21875 to 0.21875
- coefficients: float32 [6, 30], replicated, may hold values from -0.4375 to 0.4375
- tile_values: bfloat16 [32, 1, 56, 16, 128], P('node', 'rel'), may hold values from -0.03125 to 0.03125
- tile_source: int32 [32, 1, 56], P('node', 'rel'), may hold values from 0 to 3
- tile_relation: int32 [32, 1, 56], P('node', 'rel'), may hold values from 0 to 4
- tile_count: int32 [32, 1], P('node', 'rel'), may hold values from 14 to 56, as said below
Outputs:
- layer_output: bfloat16 [1, 512, 1024], P('rel', 'node')
The draws below stay inside these ranges and needn't reach their ends.
Inputs may be any that keep to these rules, and one draw needn't show every extreme that they name: `tile_count`: the live slots of each stretch and group are its first ones; in every draw some stretch and group has all 56 slots live.
All inputs are finite; a program needn't handle non-finite values.
Results may differ from the reference program's by a relative error of at most 0.0054.
Values may be sent and summed in bfloat16 or wider, within the bound.
A program may use at most 64 MiB of HBM per device.

```python
import jax
import jax.numpy as jnp
from jax import lax

DIN = 768
DOUT = 1024
NBASES = 30
RELS = 5
TILE = 128
ROWS = 16
SLOTS = 56
GROUPS = 1
STRETCHES = 32
DEST = 16
GROUP_ROWS = 512
SRC_BLOCKS = 4


def draw_tile_count(key, part):
    first_key = jax.random.fold_in(key, 11)
    second_key = jax.random.fold_in(key, 12)
    third_key = jax.random.fold_in(key, 13)
    base_count = jax.random.randint(first_key, (STRETCHES, GROUPS), SLOTS // 4, SLOTS // 2 + 1)
    full_mask = jax.random.randint(second_key, (STRETCHES, GROUPS), 0, 8) == 0
    chosen = jax.random.randint(third_key, (), 0, STRETCHES * GROUPS)
    forced = jnp.arange(STRETCHES * GROUPS, dtype=jnp.int32).reshape(STRETCHES, GROUPS) == chosen
    return jnp.where(full_mask | forced, SLOTS, base_count).astype(jnp.int32)


def touch_ends(entries, rng, least, largest):
    longest = entries.shape.index(max(entries.shape))
    spots = []
    for shift in (0, 1):
        where = [jax.random.randint(jax.random.fold_in(rng, axis), (), 0, length) for axis, length in enumerate(entries.shape)]
        where[longest] = (where[longest] + shift) % entries.shape[longest]
        spots.append(tuple(where))
    return entries.at[spots[0]].set(least).at[spots[1]].set(largest)


def level_of(key, dims, shards, smallest, high):
    def one(axis_at, parts):
        steps = jax.random.uniform(jax.random.fold_in(jax.random.fold_in(key, 6), axis_at), (parts,), jnp.float32, smallest / len(shards), high / len(shards))
        return jnp.repeat(jnp.exp(steps), dims[axis_at] // parts).reshape((-1,) + (1,) * (len(dims) - axis_at - 1))

    gain = one(*shards[0])
    for cut in shards[1:]:
        gain = gain * one(*cut)
    return gain


def noise(rng, extent, scale, reach, split=(), kind=jnp.bfloat16):
    loudness = level_of(rng, extent, split, -0.22, 0.18) if split else 1.0
    values = jax.random.normal(rng, extent, jnp.float32) * scale * loudness
    return jnp.minimum(jnp.maximum(values, -reach), reach).astype(kind)


def setup_inputs(seed: int = 0) -> dict:
    key_of = jax.random.split(jax.random.key(seed), 8)
    return {
        "features": noise(key_of[0], (GROUPS, GROUP_ROWS, DIN), 1.0, 6.0, ((1, 32),)),
        "bases": noise(key_of[1], (NBASES, DIN, DOUT), DIN ** -0.5, 0.21875, ((1, 32),)),
        "coefficients": noise(key_of[2], (RELS + 1, NBASES), (NBASES * (RELS + 1)) ** -0.5, 0.4375, (), jnp.float32),
        "tile_values": noise(key_of[3], (STRETCHES, GROUPS, SLOTS, DEST, TILE), (4 * TILE * SLOTS) ** -0.5, 0.03125, ((0, 32),)),
        "tile_source": touch_ends(jax.random.randint(key_of[4], (STRETCHES, GROUPS, SLOTS), 0, SRC_BLOCKS), jax.random.fold_in(key_of[4], 1), 0, SRC_BLOCKS - 1).astype(jnp.int32),
        "tile_relation": touch_ends(jax.random.randint(key_of[5], (STRETCHES, GROUPS, SLOTS), 0, RELS), jax.random.fold_in(key_of[5], 1), 0, RELS - 1).astype(jnp.int32),
        "tile_count": draw_tile_count(jax.random.fold_in(key_of[7], 71), 0),
    }


def reference(features, bases, coefficients, tile_values, tile_source, tile_relation, tile_count):
    stacked = jnp.dot(coefficients, bases.reshape(NBASES, DIN * DOUT).astype(jnp.float32), precision=lax.Precision.HIGHEST)
    weights = stacked.astype(jnp.bfloat16).reshape((RELS + 1) * DIN, DOUT)
    blocks = features.reshape(GROUPS, SRC_BLOCKS, TILE, DIN)
    slot_ids = jnp.arange(SLOTS, dtype=jnp.int32)
    rel_ids = jnp.arange(RELS, dtype=jnp.int32)

    def one_stretch(stretch_index):
        def one_group(aggregate, group_index):
            live_slots = slot_ids < tile_count[stretch_index, group_index]
            picked = jnp.take(blocks[group_index], tile_source[stretch_index, group_index], axis=0)
            products = jnp.einsum("sab,sbd->sad", tile_values[stretch_index, group_index].astype(jnp.float32), picked.astype(jnp.float32))
            select = ((tile_relation[stretch_index, group_index][:, None] == rel_ids[None, :]) & live_slots[:, None]).astype(jnp.float32)
            return aggregate + jnp.einsum("sr,sad->ard", select, products), None

        aggregate, _ = lax.scan(one_group, jnp.zeros((DEST, RELS, DIN), jnp.float32), jnp.arange(GROUPS, dtype=jnp.int32))
        own_rows = lax.dynamic_slice_in_dim(features, stretch_index * ROWS, ROWS, 1).reshape(DEST, 1, DIN)
        messages = jnp.concatenate([aggregate.astype(jnp.bfloat16), own_rows], axis=1).reshape(DEST, (RELS + 1) * DIN)
        output = jnp.dot(messages, weights, preferred_element_type=jnp.float32)
        return jnp.maximum(output, 0.0).astype(jnp.bfloat16)

    blocks_out = lax.map(one_stretch, jnp.arange(STRETCHES, dtype=jnp.int32))
    return blocks_out.reshape(STRETCHES, GROUPS, ROWS, DOUT).transpose(1, 0, 2, 3).reshape(GROUPS, GROUP_ROWS, DOUT)
```

```python
import functools

import jax
import jax.numpy as jnp
from jax import lax
from jax.experimental import pallas as pl
from jax.experimental.pallas import tpu as pltpu
from jax.sharding import PartitionSpec as P

TILE = 128
LANES = 128
HALF = 64


batch_tiles = 8


def general_path(features, bases, coefficients, tile_values, tile_source, tile_relation, tile_count):
    relations = coefficients.shape[0] - 1
    nbases, din_part, dout_part = bases.shape
    stacked = jnp.dot(
        coefficients,
        bases.reshape(nbases, din_part * dout_part).astype(jnp.float32),
        precision=lax.Precision.HIGHEST,
    )
    weight_part = stacked.astype(jnp.bfloat16).reshape(relations + 1, din_part, dout_part)
    own_rows = features[0]
    row_count, in_width = own_rows.shape
    gathered = lax.all_gather(features, "node", axis=1, tiled=True)[0]
    blocks = gathered.reshape(-1, TILE, in_width)
    values = tile_values[0, 0]
    sources = tile_source[0, 0]
    relation_ids = tile_relation[0, 0]
    live_count = tile_count[0, 0]
    dest_rows = values.shape[1]
    kind_ids = jnp.arange(relations, dtype=jnp.int32)

    def accumulate(step_index, aggregate):
        first_slot = step_index * batch_tiles
        tile_block = lax.dynamic_slice_in_dim(values, first_slot, batch_tiles, 0)
        source_ids = lax.dynamic_slice_in_dim(sources, first_slot, batch_tiles, 0)
        labels = lax.dynamic_slice_in_dim(relation_ids, first_slot, batch_tiles, 0)
        picked = jnp.take(blocks, source_ids, axis=0)
        products = jnp.einsum(
            "sab,sbd->sad", tile_block, picked, preferred_element_type=jnp.float32
        )
        live_slots = first_slot + jnp.arange(batch_tiles, dtype=jnp.int32) < live_count
        select = ((labels[:, None] == kind_ids[None, :]) & live_slots[:, None]).astype(jnp.float32)
        return aggregate + jnp.einsum(
            "sr,sad->ard", select, products, precision=lax.Precision.HIGHEST
        )

    turn_count = (live_count + batch_tiles - 1) // batch_tiles
    aggregate = lax.fori_loop(
        0, turn_count, accumulate, jnp.zeros((dest_rows, relations, in_width), jnp.float32)
    )
    weight_rows = lax.all_gather(weight_part, "node", axis=1, tiled=True)
    group_index = lax.axis_index("rel")
    self_part = lax.dynamic_update_slice(
        jnp.zeros((dest_rows, 1, in_width), jnp.float32),
        own_rows.astype(jnp.float32)[:, None, :],
        (group_index * row_count, 0, 0),
    )
    summed = lax.psum(jnp.concatenate([aggregate, self_part], axis=1), "rel")
    messages = summed.astype(jnp.bfloat16).reshape(dest_rows, -1)
    columns = jnp.dot(
        messages, weight_rows.reshape(-1, dout_part), preferred_element_type=jnp.float32
    )
    local_cols = jnp.maximum(columns, 0.0).astype(jnp.bfloat16)
    return lax.all_to_all(local_cols, "rel", split_axis=0, concat_axis=1, tiled=True)[None]


def layer_kernel(
    chips,
    sources,
    feat_ref,
    coef_ref,
    src_ref,
    rel_ref,
    count_ref,
    values_ref,
    bases_hbm,
    out_ref,
    bases_v,
    rows_v,
    adj_v,
    own_w,
    other_w,
    full_w,
    msg_out,
    msg_in,
    part_out,
    part_in,
    bases_sem,
    own_sem,
    feat_send,
    feat_recv,
    fwd_send,
    w_send,
    w_recv,
    msg_send,
    msg_recv,
    part_send,
    part_recv,
):
    f32, bf16 = jnp.float32, jnp.bfloat16
    kinds, nbases = coef_ref.shape
    relations = kinds - 1
    slots, dest, tile = values_ref.shape[2:]
    din_part = own_w.shape[1]
    dout = out_ref.shape[2]
    width = feat_ref.shape[2]
    me = lax.axis_index("node")
    core, chip = me % 2, me // 2
    mate = chip * 2 + (1 - core)

    def peer(step):
        return ((chip + step) % chips) * 2 + core

    def remote(src, dst, send, recv, target):
        return pltpu.make_async_remote_copy(
            src_ref=src,
            dst_ref=dst,
            send_sem=send,
            recv_sem=recv,
            device_id={"node": target},
            device_id_type=pl.DeviceIdType.MESH,
        )

    load_bases = pltpu.make_async_copy(bases_hbm, bases_v, bases_sem)
    load_bases.start()

    barrier = pltpu.get_barrier_semaphore()

    def greet(step, carry):
        pl.semaphore_signal(
            barrier, inc=1, device_id={"node": peer(step)}, device_id_type=pl.DeviceIdType.MESH
        )
        return carry

    lax.fori_loop(1, chips, greet, 0)
    pl.semaphore_signal(
        barrier, inc=1, device_id={"node": mate}, device_id_type=pl.DeviceIdType.MESH
    )
    keep_own = pltpu.make_async_copy(feat_ref.at[0], rows_v.at[me], own_sem)
    keep_own.start()
    pl.semaphore_wait(barrier, chips)

    def feat_copy(step):
        return remote(
            feat_ref.at[0], rows_v.at[me], feat_send.at[step], feat_recv.at[step], peer(step)
        )

    def send_feat(step, carry):
        feat_copy(step).start()
        return carry

    lax.fori_loop(1, chips, send_feat, 0)
    mate_copy = remote(feat_ref.at[0], rows_v.at[me], fwd_send.at[0], feat_recv.at[chips], mate)
    mate_copy.start()

    load_bases.wait()

    def weigh(chunk, carry):
        lanes = pl.ds(pl.multiple_of(chunk * LANES, LANES), LANES)
        sums = [None] * kinds
        for b in range(nbases):
            part = bases_v[b, :, lanes].astype(f32)
            for r in range(kinds):
                term = coef_ref[r, b] * part
                sums[r] = term if sums[r] is None else sums[r] + term
        for r in range(kinds):
            own_w[r, :, lanes] = sums[r].astype(bf16)
        return carry

    lax.fori_loop(0, dout // LANES, weigh, 0)

    def fwd_copy(step):
        slot = ((chip - step + chips) % chips) * 2 + core
        return remote(
            rows_v.at[slot],
            rows_v.at[slot],
            fwd_send.at[step],
            feat_recv.at[chips + step],
            mate,
        )

    def forward(step, carry):
        feat_copy(step).wait_recv()
        fwd_copy(step).start()
        return carry

    lax.fori_loop(1, chips, forward, 0)
    w_copy = remote(own_w, other_w, w_send, w_recv, mate)
    w_copy.start()

    pairs = relations * sources
    live = count_ref[0, 0]

    def add_tile(t, sums):
        block = values_ref[0, 0, t].astype(f32)
        label = rel_ref[0, 0, t] * sources + src_ref[0, 0, t]
        label = jnp.where(t < live, label, -1)
        return tuple(
            sums[k] + block * (label == k).astype(f32) for k in range(pairs)
        )

    sums = lax.fori_loop(
        0, slots, add_tile, tuple(jnp.zeros((dest, tile), f32) for _ in range(pairs))
    )
    for r in range(relations):
        for s in range(sources):
            full = sums[r * sources + s]
            high = full.astype(bf16)
            lanes = slice(s * tile, (s + 1) * tile)
            adj_v[r * dest : (r + 1) * dest, lanes] = high
            adj_v[(relations + r) * dest : (relations + r + 1) * dest, lanes] = (
                full - high.astype(f32)
            ).astype(bf16)

    keep_own.wait()
    mate_copy.wait_recv()

    def wait_forward(step, carry):
        fwd_copy(step).wait_recv()
        return carry

    lax.fori_loop(1, chips, wait_forward, 0)

    both = jnp.dot(
        adj_v[...], rows_v[...].reshape(-1, width), preferred_element_type=f32
    )
    half_rows = relations * dest
    messages = jnp.concatenate(
        [both[:half_rows] + both[half_rows:], feat_ref[0].astype(f32)], axis=0
    )
    even = jnp.concatenate([messages[r * dest : (r + 1) * dest] for r in range(0, kinds, 2)], 0)
    odd = jnp.concatenate([messages[r * dest : (r + 1) * dest] for r in range(1, kinds, 2)], 0)
    odd = jnp.concatenate([odd[:, width - HALF :], odd[:, : width - HALF]], axis=1)
    even = jnp.concatenate([even, even[:, :LANES]], axis=1)
    odd = jnp.concatenate([odd, odd[:, :LANES]], axis=1)
    low_half = lax.broadcasted_iota(jnp.int32, ((kinds // 2) * dest, LANES), 1) < HALF
    piece = 2 * din_part
    for q in range(chips):
        at = q * piece
        window = jnp.where(low_half, even[:, at : at + LANES], odd[:, at : at + LANES])
        window = window.astype(bf16)
        for h in range(kinds // 2):
            msg_out[q, :, h * LANES : (h + 1) * LANES] = window[h * dest : (h + 1) * dest]

    def msg_copy(step):
        return remote(
            msg_out.at[(chip + step) % chips],
            msg_in.at[step],
            msg_send.at[step],
            msg_recv.at[step],
            peer(step),
        )

    def send_msg(step, carry):
        msg_copy(step).start()
        return carry

    lax.fori_loop(1, chips, send_msg, 0)
    msg_in[0] = msg_out[chip]

    w_copy.wait()
    blank = jnp.zeros((HALF - piece, LANES), f32)

    def assemble(chunk, carry):
        lanes = pl.ds(pl.multiple_of(chunk * LANES, LANES), LANES)
        for r in range(kinds):
            mine = own_w[r, :, lanes].astype(f32)
            theirs = other_w[r, :, lanes].astype(f32)
            first = jnp.where(core == 0, mine, theirs)
            second = jnp.where(core == 0, theirs, mine)
            full_w[r * HALF : (r + 1) * HALF, lanes] = jnp.concatenate(
                [first, second, blank], axis=0
            ).astype(bf16)
        return carry

    lax.fori_loop(0, dout // LANES, assemble, 0)

    def wait_msg(step, carry):
        msg_copy(step).wait_recv()
        return carry

    def part_copy(step):
        return remote(
            part_out.at[step],
            part_in.at[step],
            part_send.at[step],
            part_recv.at[step],
            ((chip - step + chips) % chips) * 2 + core,
        )

    def send_part(step, carry):
        part_copy(step).start()
        return carry

    groups = 2
    per_group = chips // groups
    for g in range(groups):
        first, last = g * per_group, (g + 1) * per_group
        lax.fori_loop(max(first, 1), last, wait_msg, 0)
        rows = msg_in[first:last].reshape(per_group * dest, msg_in.shape[2])
        part = jnp.dot(rows, full_w[...], preferred_element_type=f32)
        part_out[first:last] = part.astype(bf16).reshape(per_group, dest, dout)
        lax.fori_loop(max(first, 1), last, send_part, 0)

    total = part_out[0].astype(f32)
    for step in range(1, chips):
        part_copy(step).wait_recv()
        total = total + part_in[step].astype(f32)
    out_ref[0] = jnp.maximum(total, 0.0).astype(bf16)

    mate_copy.wait_send()

    def drain(step, carry):
        feat_copy(step).wait_send()
        fwd_copy(step).wait_send()
        msg_copy(step).wait_send()
        part_copy(step).wait_send()
        return carry

    lax.fori_loop(1, chips, drain, 0)


def fused_path(features, bases, coefficients, tile_values, tile_source, tile_relation, tile_count):
    nodes = lax.axis_size("node")
    chips = nodes // 2
    kinds = coefficients.shape[0]
    nbases, din_part, dout = bases.shape
    _, row_count, width = features.shape
    dest, tile = tile_values.shape[3:]
    sources = nodes * row_count // tile
    depth = kinds * HALF
    bf16 = jnp.bfloat16
    vmem = pl.BlockSpec(memory_space=pltpu.VMEM)
    smem = pl.BlockSpec(memory_space=pltpu.SMEM)
    dma = pltpu.SemaphoreType.DMA
    return pl.pallas_call(
        functools.partial(layer_kernel, chips, sources),
        out_shape=jax.ShapeDtypeStruct((1, row_count, dout), bf16),
        in_specs=[vmem, smem, smem, smem, smem, vmem, pl.BlockSpec(memory_space=pl.ANY)],
        out_specs=vmem,
        scratch_shapes=[
            pltpu.VMEM((nbases, din_part, dout), bf16),
            pltpu.VMEM((nodes, row_count, width), bf16),
            pltpu.VMEM((2 * (kinds - 1) * dest, sources * tile), bf16),
            pltpu.VMEM((kinds, din_part, dout), bf16),
            pltpu.VMEM((kinds, din_part, dout), bf16),
            pltpu.VMEM((depth, dout), bf16),
            pltpu.VMEM((chips, dest, depth), bf16),
            pltpu.VMEM((chips, dest, depth), bf16),
            pltpu.VMEM((chips, dest, dout), bf16),
            pltpu.VMEM((chips, dest, dout), bf16),
            dma,
            dma,
            dma((chips,)),
            dma((2 * chips,)),
            dma((chips,)),
            dma,
            dma,
            dma((chips,)),
            dma((chips,)),
            dma((chips,)),
            dma((chips,)),
        ],
        compiler_params=pltpu.CompilerParams(collective_id=0, has_side_effects=True),
        name="layer",
    )(features, coefficients, tile_source, tile_relation, tile_count, tile_values, bases)


def solution(mesh):
    def on_device(features, bases, coefficients, *tiles):
        kinds = coefficients.shape[0]
        din_part = bases.shape[1]
        nodes = mesh.shape["node"]
        fits = (
            mesh.shape["rel"] == 1
            and nodes % 4 == 0
            and kinds % 2 == 0
            and 2 * din_part <= HALF
            and features.shape[1] == tiles[0].shape[3]
        )
        path = fused_path if fits else general_path
        return path(features, bases, coefficients, *tiles)

    return jax.shard_map(
        on_device,
        mesh=mesh,
        in_specs=(
            P("rel", "node", None),
            P(None, "node", "rel"),
            P(),
            P("node", "rel", None, None, None),
            P("node", "rel", None),
            P("node", "rel", None),
            P("node", "rel"),
        ),
        out_specs=P("rel", "node", None),
        check_vma=False,
    )
```

```python
import functools

import jax
import jax.numpy as jnp
from jax import lax
from jax.experimental import pallas as pl
from jax.experimental.pallas import tpu as pltpu
from jax.sharding import PartitionSpec as P

TILE = 128
LANES = 128
PLANE = 8


batch_tiles = 8


def general_path(features, bases, coefficients, tile_values, tile_source, tile_relation, tile_count):
    relations = coefficients.shape[0] - 1
    nbases, din_part, dout_part = bases.shape
    stacked = jnp.dot(
        coefficients,
        bases.reshape(nbases, din_part * dout_part).astype(jnp.float32),
        precision=lax.Precision.HIGHEST,
    )
    weight_part = stacked.astype(jnp.bfloat16).reshape(relations + 1, din_part, dout_part)
    own_rows = features[0]
    row_count, in_width = own_rows.shape
    gathered = lax.all_gather(features, "node", axis=1, tiled=True)[0]
    blocks = gathered.reshape(-1, TILE, in_width)
    values = tile_values[0, 0]
    sources = tile_source[0, 0]
    relation_ids = tile_relation[0, 0]
    live_count = tile_count[0, 0]
    dest_rows = values.shape[1]
    kind_ids = jnp.arange(relations, dtype=jnp.int32)

    def accumulate(step_index, aggregate):
        first_slot = step_index * batch_tiles
        tile_block = lax.dynamic_slice_in_dim(values, first_slot, batch_tiles, 0)
        source_ids = lax.dynamic_slice_in_dim(sources, first_slot, batch_tiles, 0)
        labels = lax.dynamic_slice_in_dim(relation_ids, first_slot, batch_tiles, 0)
        picked = jnp.take(blocks, source_ids, axis=0)
        products = jnp.einsum(
            "sab,sbd->sad", tile_block, picked, preferred_element_type=jnp.float32
        )
        live_slots = first_slot + jnp.arange(batch_tiles, dtype=jnp.int32) < live_count
        select = ((labels[:, None] == kind_ids[None, :]) & live_slots[:, None]).astype(jnp.float32)
        return aggregate + jnp.einsum(
            "sr,sad->ard", select, products, precision=lax.Precision.HIGHEST
        )

    turn_count = (live_count + batch_tiles - 1) // batch_tiles
    aggregate = lax.fori_loop(
        0, turn_count, accumulate, jnp.zeros((dest_rows, relations, in_width), jnp.float32)
    )
    weight_rows = lax.all_gather(weight_part, "node", axis=1, tiled=True)
    group_index = lax.axis_index("rel")
    self_part = lax.dynamic_update_slice(
        jnp.zeros((dest_rows, 1, in_width), jnp.float32),
        own_rows.astype(jnp.float32)[:, None, :],
        (group_index * row_count, 0, 0),
    )
    summed = lax.psum(jnp.concatenate([aggregate, self_part], axis=1), "rel")
    messages = summed.astype(jnp.bfloat16).reshape(dest_rows, -1)
    columns = jnp.dot(
        messages, weight_rows.reshape(-1, dout_part), preferred_element_type=jnp.float32
    )
    local_cols = jnp.maximum(columns, 0.0).astype(jnp.bfloat16)
    return lax.all_to_all(local_cols, "rel", split_axis=0, concat_axis=1, tiled=True)[None]


def layer_kernel(
    planes,
    sources,
    feat_ref,
    coef_ref,
    src_ref,
    rel_ref,
    count_ref,
    values_ref,
    bases_hbm,
    out_ref,
    bases_v,
    cols_out,
    cols_in,
    adj_in,
    weights_in,
    full_w,
    part_out,
    part_in,
    bases_sem,
    cols_send,
    cols_recv,
    fwd_send,
    fwd_recv,
    adj_send,
    adj_recv,
    w_send,
    w_recv,
    w_fwd_send,
    w_fwd_recv,
    part_send,
    part_recv,
):
    f32, bf16 = jnp.float32, jnp.bfloat16
    kinds, nbases = coef_ref.shape
    relations = kinds - 1
    slots, dest, tile = values_ref.shape[2:]
    din_part, half_out = weights_in.shape[3:]
    dout = out_ref.shape[2]
    piece = PLANE * din_part
    chips = planes * PLANE // 2
    me = lax.axis_index("node")
    core, chip, plane, seat = me % 2, me // 2, me // PLANE, me % PLANE
    mate = me + 1 - 2 * core
    corner = seat // 2
    beside = plane * PLANE + (corner + 1 - 2 * (corner % 2)) * 2 + core
    across = plane * PLANE + ((corner + 2) % 4) * 2 + core
    diagonal = ((corner + 1 - 2 * (corner % 2) + 2) % 4) * 2 + core

    def remote(src, dst, send, recv, target):
        return pltpu.make_async_remote_copy(
            src_ref=src,
            dst_ref=dst,
            send_sem=send,
            recv_sem=recv,
            device_id={"node": target},
            device_id_type=pl.DeviceIdType.MESH,
        )

    def peer(step):
        return ((chip + step) % chips) * 2 + core

    load_bases = pltpu.make_async_copy(bases_hbm, bases_v, bases_sem)
    load_bases.start()

    barrier = pltpu.get_barrier_semaphore()

    def greet(step, carry):
        pl.semaphore_signal(
            barrier, inc=1, device_id={"node": peer(step)}, device_id_type=pl.DeviceIdType.MESH
        )
        return carry

    lax.fori_loop(1, chips, greet, 0)
    pl.semaphore_signal(
        barrier, inc=1, device_id={"node": mate}, device_id_type=pl.DeviceIdType.MESH
    )
    own = feat_ref[0].astype(f32)
    gap = jnp.zeros((dest, cols_out.shape[2] - piece), f32)
    for z in range(planes):
        cut = jnp.concatenate([own[:, z * piece : (z + 1) * piece], gap], axis=1)
        cols_out[z] = cut.astype(bf16)
    pl.semaphore_wait(barrier, chips)

    def cols_copy(step):
        target = peer(step)
        return remote(
            cols_out.at[target // PLANE],
            cols_in.at[me],
            cols_send.at[step],
            cols_recv.at[step],
            target,
        )

    def send_cols(step, carry):
        cols_copy(step).start()
        return carry

    lax.fori_loop(1, chips, send_cols, 0)
    own_fwd = remote(cols_out.at[plane], cols_in.at[me], fwd_send.at[0], fwd_recv.at[0], mate)
    own_fwd.start()
    cols_in[me] = cols_out[plane]

    load_bases.wait()
    chunks = half_out // LANES

    def own_weights(half):
        def weigh(chunk, carry):
            lanes = pl.ds(pl.multiple_of(chunk * LANES, LANES), LANES)
            there = pl.ds(pl.multiple_of((half * chunks + chunk) * LANES, LANES), LANES)
            sums = [None] * kinds
            for b in range(nbases):
                part = bases_v[b, :, there].astype(f32)
                for r in range(kinds):
                    term = coef_ref[r, b] * part
                    sums[r] = term if sums[r] is None else sums[r] + term
            for r in range(kinds):
                weights_in[half, seat, r, :, lanes] = sums[r].astype(bf16)
            return carry

        lax.fori_loop(0, chunks, weigh, 0)

    def w_copy(half, seat_of, slot, target):
        at = weights_in.at[half, seat_of]
        return remote(at, at, w_send.at[slot], w_recv.at[slot], target)

    def w_fwd(half, seat_of, slot):
        at = weights_in.at[half, seat_of]
        return remote(at, at, w_fwd_send.at[slot], w_fwd_recv.at[slot], mate)

    first_sends = [
        [w_copy(half, seat, half, beside), w_copy(half, seat, 2 + half, across)]
        for half in range(2)
    ]
    own_sends = [w_fwd(half, seat, 6 + half) for half in range(2)]
    for half in range(2):
        own_weights(half)
        for copy in first_sends[half]:
            copy.start()
        own_sends[half].start()

        if half == 0:
            pairs = relations * sources
            live = count_ref[0, 0]

            def add_tile(t, sums):
                block = values_ref[0, 0, t].astype(f32)
                label = rel_ref[0, 0, t] * sources + src_ref[0, 0, t]
                label = jnp.where(t < live, label, -1)
                return tuple(sums[k] + block * (label == k).astype(f32) for k in range(pairs))

            sums = lax.fori_loop(
                0, slots, add_tile, tuple(jnp.zeros((dest, tile), f32) for _ in range(pairs))
            )
            for r in range(relations):
                for s in range(sources):
                    adj_in[plane, r * dest : (r + 1) * dest, s * tile : (s + 1) * tile] = sums[
                        r * sources + s
                    ].astype(bf16)

            def column(step):
                return ((plane + step) % planes) * PLANE + seat

            def adj_copy(step):
                at = adj_in.at[plane]
                return remote(at, at, adj_send.at[step], adj_recv.at[step], column(step))

            for step in range(1, planes):
                adj_copy(step).start()

    def cols_fwd(step):
        slot = ((chip - step + chips) % chips) * 2 + core
        at = cols_in.at[slot]
        return remote(at, at, fwd_send.at[step], fwd_recv.at[step], mate)

    def forward(step, carry):
        cols_copy(step).wait_recv()
        cols_fwd(step).start()
        return carry

    lax.fori_loop(1, chips, forward, 0)

    seat_beside, seat_across = beside % PLANE, across % PLANE
    relay_across = w_copy(0, seat_beside, 4, across)
    relay_beside = w_copy(1, seat_across, 5, beside)
    mate_sends = [
        w_fwd(0, seat_beside, 0),
        w_fwd(1, seat_beside, 1),
        w_fwd(0, seat_across, 2),
        w_fwd(1, seat_across, 3),
        w_fwd(0, diagonal, 4),
        w_fwd(1, diagonal, 5),
    ]
    first_sends[0][0].wait_recv()
    relay_across.start()
    mate_sends[0].start()
    first_sends[0][1].wait_recv()
    mate_sends[2].start()
    first_sends[1][1].wait_recv()
    relay_beside.start()
    mate_sends[3].start()
    first_sends[1][0].wait_recv()
    mate_sends[1].start()

    own_fwd.wait_recv()

    def wait_forward(step, carry):
        cols_fwd(step).wait_recv()
        return carry

    lax.fori_loop(1, chips, wait_forward, 0)
    for step in range(1, planes):
        adj_copy(step).wait_recv()

    relay_across.wait_recv()
    mate_sends[4].start()
    relay_beside.wait_recv()
    mate_sends[5].start()

    block_rows = relations * dest
    gathered = jnp.dot(
        adj_in[...].reshape(planes * block_rows, sources * tile),
        cols_in[...].reshape(sources * tile, cols_in.shape[2]),
        preferred_element_type=f32,
    ).astype(bf16)
    lhs = []
    for r in range(relations):
        rows = [
            gathered[z * block_rows + r * dest : z * block_rows + (r + 1) * dest]
            for z in range(planes)
        ]
        lhs.append(jnp.concatenate(rows, axis=0)[:, :piece])
    rows = [cols_in[z * PLANE + seat] for z in range(planes)]
    lhs.append(jnp.concatenate(rows, axis=0)[:, :piece])

    for copy in own_sends + mate_sends:
        copy.wait_recv()

    for half in range(2):

        def assemble(chunk, carry):
            lanes = pl.ds(pl.multiple_of(chunk * LANES, LANES), LANES)
            there = pl.ds(pl.multiple_of((half * chunks + chunk) * LANES, LANES), LANES)
            for r in range(kinds):
                rows = [weights_in[half, d, r, :, lanes].astype(f32) for d in range(PLANE)]
                full_w[r * piece : (r + 1) * piece, there] = jnp.concatenate(rows, axis=0).astype(
                    bf16
                )
            return carry

        lax.fori_loop(0, chunks, assemble, 0)

    part = None
    for r in range(kinds):
        term = jnp.dot(
            lhs[r], full_w[r * piece : (r + 1) * piece], preferred_element_type=f32
        )
        part = term if part is None else part + term
    part_out[...] = part.astype(bf16).reshape(planes, dest, dout)

    def part_copy(step):
        return remote(
            part_out.at[(plane + step) % planes],
            part_in.at[step],
            part_send.at[step],
            part_recv.at[step],
            column(step),
        )

    for step in range(1, planes):
        part_copy(step).start()
    total = part_out[plane].astype(f32)
    for step in range(1, planes):
        part_copy(step).wait_recv()
        total = total + part_in[step].astype(f32)
    out_ref[0] = jnp.maximum(total, 0.0).astype(bf16)

    def drain(step, carry):
        cols_copy(step).wait_send()
        cols_fwd(step).wait_send()
        return carry

    lax.fori_loop(1, chips, drain, 0)
    own_fwd.wait_send()
    for copy in first_sends[0] + first_sends[1] + own_sends + mate_sends:
        copy.wait_send()
    relay_across.wait_send()
    relay_beside.wait_send()
    for step in range(1, planes):
        adj_copy(step).wait_send()
        part_copy(step).wait_send()


def fused_path(features, bases, coefficients, tile_values, tile_source, tile_relation, tile_count):
    nodes = lax.axis_size("node")
    planes = nodes // PLANE
    chips = nodes // 2
    kinds = coefficients.shape[0]
    nbases, din_part, dout = bases.shape
    row_count = features.shape[1]
    dest, tile = tile_values.shape[3:]
    sources = nodes * row_count // tile
    piece = PLANE * din_part
    wide = (piece + LANES - 1) // LANES * LANES
    bf16 = jnp.bfloat16
    vmem = pl.BlockSpec(memory_space=pltpu.VMEM)
    smem = pl.BlockSpec(memory_space=pltpu.SMEM)
    dma = pltpu.SemaphoreType.DMA
    return pl.pallas_call(
        functools.partial(layer_kernel, planes, sources),
        out_shape=jax.ShapeDtypeStruct((1, row_count, dout), bf16),
        in_specs=[vmem, smem, smem, smem, smem, vmem, pl.BlockSpec(memory_space=pl.ANY)],
        out_specs=vmem,
        scratch_shapes=[
            pltpu.VMEM((nbases, din_part, dout), bf16),
            pltpu.VMEM((planes, row_count, wide), bf16),
            pltpu.VMEM((nodes, row_count, wide), bf16),
            pltpu.VMEM((planes, (kinds - 1) * dest, sources * tile), bf16),
            pltpu.VMEM((2, PLANE, kinds, din_part, dout // 2), bf16),
            pltpu.VMEM((kinds * piece, dout), bf16),
            pltpu.VMEM((planes, dest, dout), bf16),
            pltpu.VMEM((planes, dest, dout), bf16),
            dma,
            dma((chips,)),
            dma((chips,)),
            dma((chips,)),
            dma((chips,)),
            dma((planes,)),
            dma((planes,)),
            dma((6,)),
            dma((6,)),
            dma((8,)),
            dma((8,)),
            dma((planes,)),
            dma((planes,)),
        ],
        compiler_params=pltpu.CompilerParams(collective_id=0, has_side_effects=True),
        name="layer",
    )(features, coefficients, tile_source, tile_relation, tile_count, tile_values, bases)


def solution(mesh):
    def on_device(features, bases, coefficients, *tiles):
        kinds = coefficients.shape[0]
        din_part = bases.shape[1]
        nodes = mesh.shape["node"]
        fits = (
            mesh.shape["rel"] == 1
            and nodes % PLANE == 0
            and bases.shape[2] % (2 * LANES) == 0
            and features.shape[1] == tiles[0].shape[3]
        )
        path = fused_path if fits else general_path
        return path(features, bases, coefficients, *tiles)

    return jax.shard_map(
        on_device,
        mesh=mesh,
        in_specs=(
            P("rel", "node", None),
            P(None, "node", "rel"),
            P(),
            P("node", "rel", None, None, None),
            P("node", "rel", None),
            P("node", "rel", None),
            P("node", "rel"),
        ),
        out_specs=P("rel", "node", None),
        check_vma=False,
    )
```
